32 devices in a mesh: img: 8 (over y, x, core), head: 4 (over z).
Axes of the slice: x: 2, y: 2, z: 4, core: 2. Of those that a mesh axis runs over, the one named last changes fastest.
Arguments:
- latents: bfloat16 [192, 64, 1024], P('img'), may hold values from -6 to 6
- media: bfloat16 [192, 256, 1024], P('img'), may hold values from -6 to 6
- valid_counts: int32 [192], P('img'), may hold values from 160 to 256, as said below
- w_query: bfloat16 [1024, 512], P(None, 'head'), may hold values from -0.1875 to 0.1875
- w_key: bfloat16 [1024, 512], P(None, 'head'), may hold values from -0.1875 to 0.1875
- w_value: bfloat16 [1024, 512], P(None, 'head'), may hold values from -0.1875 to 0.1875
- w_out: bfloat16 [1024, 512], P(None, 'head'), may hold values from -2 to 2
- w_up: bfloat16 [1024, 4096], P(None, 'head'), may hold values from -0.1875 to 0.1875
- w_down: bfloat16 [1024, 4096], P(None, 'head'), may hold values from -0.09375 to 0.09375
- norm_gains: float32 [3, 1024], replicated, may hold values from 0.5 to 1.5
- norm_biases: float32 [3, 1024], replicated, may hold values from -1.8 to 1.8
- cotangent: bfloat16 [192, 64, 1024], P('img'), may hold values from -6 to 6
Outputs:
- latents_out: bfloat16 [192, 64, 1024], P('img')
- latents_grad: bfloat16 [192, 64, 1024], P('img', 'head')
- media_grad: bfloat16 [192, 256, 1024], P('img', 'head')
- w_query_grad: float32 [1024, 512], P('img', 'head')
- w_key_grad: float32 [1024, 512], P('img', 'head')
- w_value_grad: float32 [1024, 512], P('img', 'head')
- w_out_grad: float32 [1024, 512], P('img', 'head')
- w_up_grad: float32 [1024, 4096], P('img', 'head')
- w_down_grad: float32 [1024, 4096], P('img', 'head')
- norm_gains_grad: float32 [3, 1024], P(None, ('img', 'head'))
- norm_biases_grad: float32 [3, 1024], P(None, ('img', 'head'))
The draws below stay inside these ranges and needn't reach their ends.
Inputs may be any that keep to these rules, and one draw needn't show every extreme that they name: An image's valid patch keys are its first valid_counts patches; some image has exactly 256 and some exactly 160.
All inputs are finite; a program needn't handle non-finite values.
Results may differ from the reference program's by a relative error of at most 0.018.
Values may be sent and summed in bfloat16 or wider, within the bound.
No kernel may reach another device: no remote copies, remote signals or barrier semaphores. Data moves between devices by JAX's collectives and lax.ppermute only.
A program may use at most 192 MiB of HBM per device.

```python
import math
import jax
import jax.numpy as jnp
from jax import lax

D = 1024
HEADS = 8
HEAD_DIM = 64
FF = 4096
LAT = 64
PATCH = 256
HD = 512
IMAGES = 192


def draw_valid_counts(key, part):
    lowest = PATCH * 5 // 8
    key_counts, key_high, key_low = jax.random.split(jax.random.fold_in(key, 17), 3)
    counts = jax.random.randint(key_counts, (IMAGES,), lowest, PATCH + 1)
    high_image = jax.random.randint(key_high, (), 0, IMAGES)
    low_image = (high_image + 1 + jax.random.randint(key_low, (), 0, IMAGES - 1)) % IMAGES
    index_row = lax.iota(jnp.int32, IMAGES)
    counts = jnp.where(index_row == high_image, PATCH, counts)
    counts = jnp.where(index_row == low_image, lowest, counts)
    return counts.astype(jnp.int32)


def spiked(drawn, stream_key, source, target, shards_of, factor):
    def block_of(position):
        return (jnp.arange(drawn.shape[position]) // (drawn.shape[position] // shards_of)).reshape((-1,) + (1,) * (drawn.ndim - 1 - position))

    first = jax.random.permutation(stream_key, shards_of)[block_of(target)]
    far = (block_of(target) + shards_of // 2) % shards_of
    return jnp.where((block_of(source) == first) | (block_of(source) == far), factor * drawn, drawn)


def levels(stream_key, dims, shards, least, high):
    loudness, own = 1.0, jax.random.fold_in(stream_key, 6)
    for axis_at, parts in shards:
        draws = jnp.exp(jax.random.uniform(jax.random.fold_in(own, axis_at), (parts,), jnp.float32, least / len(shards), high / len(shards)))
        loudness = loudness * jnp.repeat(draws, dims[axis_at] // parts).reshape([-1 if axis == axis_at else 1 for axis in range(len(dims))])
    return loudness


def scatter_about(rng, extent, deviation, limit, pieces=(), dtype=jnp.bfloat16):
    values = jax.random.normal(rng, extent, jnp.float32) * deviation
    if len(pieces) > 0:
        values = levels(rng, extent, pieces, -0.22, 0.18) * values
    return jnp.clip(values, min=-limit, max=limit).astype(dtype)


def heavy_noise(key, extent, scale, most, shards, heavy, kind=jnp.bfloat16):
    values = scale * jax.random.normal(key, extent, jnp.float32)
    if shards:
        values = values * levels(key, extent, shards, -0.22, 0.18)
    return jnp.clip(spiked(values, jax.random.fold_in(key, 3), *heavy), -most, most).astype(kind)


def setup_inputs(seed: int = 0) -> dict:
    streams_of = jax.random.split(jax.random.key(seed), 13)
    return {
        "latents": scatter_about(streams_of[0], (IMAGES, LAT, D), 1.0, 6.0, ((0, 8),)),
        "media": scatter_about(streams_of[1], (IMAGES, PATCH, D), 1.0, 6.0, ((0, 8),)),
        "valid_counts": draw_valid_counts(jax.random.fold_in(streams_of[12], 71), 0),
        "w_query": scatter_about(streams_of[3], (D, HD), D ** -0.5, 0.1875, ((1, 4),)),
        "w_key": scatter_about(streams_of[4], (D, HD), D ** -0.5, 0.1875, ((1, 4),)),
        "w_value": scatter_about(streams_of[5], (D, HD), D ** -0.5, 0.1875, ((1, 4),)),
        "w_out": scatter_about(streams_of[6], (D, HD), (HD // 64) ** -0.5, 2.0, ((1, 4),)),
        "w_up": scatter_about(streams_of[7], (D, FF), D ** -0.5, 0.1875, ((1, 4),)),
        "w_down": scatter_about(streams_of[8], (D, FF), FF ** -0.5, 0.09375, ((1, 4),)),
        "norm_gains": jnp.clip(1.0 + 0.1 * jax.random.normal(streams_of[9], (3, D), jnp.float32), 0.5, 1.5),
        "norm_biases": scatter_about(streams_of[10], (3, D), 0.3, 1.8, (), jnp.float32),
        "cotangent": heavy_noise(streams_of[11], (IMAGES, LAT, D), 1.0, 6.0, ((0, 8),), (0, 2, 8, 2.0)),
    }


@jax.custom_vjp
def low(v):
    return lax.optimization_barrier(v.astype(jnp.bfloat16)).astype(jnp.float32)

@jax.custom_vjp
def low_back(v):
    return v

def low_keep(v):
    return (low(v), None)

def low_pass(kept, grad):
    return (grad,)

def back_keep(v):
    return (v, None)

def back_low(kept, grad):
    return (low(grad),)
low.defvjp(low_keep, low_pass)
low_back.defvjp(back_keep, back_low)
highest = lax.Precision.HIGHEST
epsilon = 1e-05

def layer_norm(values, gain_row, bias_row):
    center = lax.optimization_barrier(jnp.mean(values, axis=-1, keepdims=True))
    centered = values - center
    spread = lax.optimization_barrier(jnp.mean(centered * centered, axis=-1, keepdims=True))
    return centered * lax.rsqrt(spread + epsilon) * gain_row + bias_row

def exact_gelu(values):
    return jax.nn.gelu(values, approximate=False)

def forward(latent_in, media_in, counts, w_query, w_key, w_value, w_out, w_up, w_down, norm_gains, norm_biases):
    per_block = latent_in.shape[0]
    media_normed = low(layer_norm(media_in, norm_gains[0], norm_biases[0]))
    latent_normed = low(layer_norm(latent_in, norm_gains[1], norm_biases[1]))
    joined = jnp.concatenate([media_normed, latent_normed], axis=1)
    queries = low(low_back(jnp.einsum('gld,de->gle', latent_normed, w_query, precision=highest)))
    key_rows = low(low_back(jnp.einsum('gkd,de->gke', joined, w_key, precision=highest)))
    value_rows = low(low_back(jnp.einsum('gkd,de->gke', joined, w_value, precision=highest)))
    queries = queries.reshape(per_block, LAT, HEADS, HEAD_DIM)
    key_rows = key_rows.reshape(per_block, PATCH + LAT, HEADS, HEAD_DIM)
    value_rows = value_rows.reshape(per_block, PATCH + LAT, HEADS, HEAD_DIM)
    positions = lax.iota(jnp.int32, PATCH + LAT)
    allowed = (positions[None, :] < counts[:, None]) | (positions[None, :] >= PATCH)
    scores = jnp.einsum('glhe,gkhe->ghlk', queries, key_rows, precision=highest) * HEAD_DIM ** (-0.5)
    scores = low_back(jnp.where(allowed[:, None, None, :], scores, -1e+30))
    attention = low(jax.nn.softmax(scores, axis=-1))
    attended = jnp.einsum('ghlk,gkhe->glhe', attention, value_rows, precision=highest)
    attended = low(low_back(attended.reshape(per_block, LAT, HEADS * HEAD_DIM)))
    residual = latent_in + low_back(jnp.einsum('gle,de->gld', attended, w_out, precision=highest))
    ffn_low = low(layer_norm(residual, norm_gains[2], norm_biases[2]))
    pre_act = low_back(jnp.einsum('gld,df->glf', ffn_low, w_up, precision=highest))
    hidden = low(exact_gelu(pre_act))
    return residual + low_back(jnp.einsum('glf,df->gld', hidden, w_down, precision=highest))

def reference(latents, media, valid_counts, w_query, w_key, w_value, w_out, w_up, w_down, norm_gains, norm_biases, cotangent):
    weights = tuple((array_in.astype(jnp.float32) for array_in in (w_query, w_key, w_value, w_out, w_up, w_down, norm_gains, norm_biases)))
    per_block = math.gcd(IMAGES, 8)
    blocks = IMAGES // per_block

    def shaped(array_in):
        return array_in.astype(jnp.float32).reshape((blocks, per_block) + array_in.shape[1:])

    def flatten(array_in):
        return array_in.reshape((IMAGES,) + array_in.shape[2:])

    def one_block(totals, inputs):
        latent_in, media_in, count_block, upstream = inputs

        def closed(latent_arg, media_arg, params):
            return forward(latent_arg, media_arg, count_block, *params)
        result, puller = jax.vjp(closed, latent_in, media_in, weights)
        grad_latent, grad_media, grad_params = puller(upstream)
        totals = jax.tree.map(jnp.add, totals, grad_params)
        return (totals, (result.astype(jnp.bfloat16), grad_latent.astype(jnp.bfloat16), grad_media.astype(jnp.bfloat16)))
    starting = jax.tree.map(jnp.zeros_like, weights)
    counts = valid_counts.reshape(blocks, per_block)
    totals, (outputs, latent_grads, media_grads) = lax.scan(one_block, starting, (shaped(latents), shaped(media), counts, shaped(cotangent)))
    return (flatten(outputs), flatten(latent_grads), flatten(media_grads), totals[0], totals[1], totals[2], totals[3], totals[4], totals[5], totals[6], totals[7])
```

```python
import jax
import jax.numpy as jnp
from jax import lax
from jax.sharding import PartitionSpec as P

HEAD_DIM = 64
epsilon = 1e-05
BF = jnp.bfloat16
F32 = jnp.float32


def layer_stats(values):
    center = jnp.mean(values, axis=-1, keepdims=True)
    centered = values - center
    spread = jnp.mean(centered * centered, axis=-1, keepdims=True)
    scale = lax.rsqrt(spread + epsilon)
    return centered * scale, scale


def layer_back(grad, gain_row, xhat, scale):
    weighted = grad * gain_row
    first = jnp.mean(weighted, axis=-1, keepdims=True)
    second = jnp.mean(weighted * xhat, axis=-1, keepdims=True)
    return (weighted - first - xhat * second) * scale


def exchange(values, axis, bit):
    count = lax.axis_size(axis)
    return lax.ppermute(values, axis, [(place, place ^ bit) for place in range(count)])


def ordered_pair(bit, mine, other, dim):
    low = jnp.where(bit == 0, mine, other)
    high = jnp.where(bit == 0, other, mine)
    return jnp.concatenate([low, high], axis=dim)


def bit_count(count):
    return count.bit_length() - 1


def gather_img(piece, order):
    bits = len(order)
    place = lax.axis_index("img")
    held = piece.reshape((1,) * bits + piece.shape)
    for bit in order:
        other = exchange(held, "img", 1 << bit)
        held = ordered_pair((place >> bit) & 1, held, other, bits - 1 - bit)
    return held.reshape((-1,) + piece.shape[1:])


def scatter_img(values, order, dim, last):
    bits = len(order)
    place = lax.axis_index("img")
    shape = values.shape
    held = values.reshape(shape[:dim] + (2,) * bits + (-1,) + shape[dim + 1 :])
    for step, bit in enumerate(order):
        mine = (place >> bit) & 1
        axis = dim + bits - 1 - bit
        keep = lax.dynamic_slice_in_dim(held, mine, 1, axis)
        send = lax.dynamic_slice_in_dim(held, 1 - mine, 1, axis)
        got = exchange(send, "img", 1 << bit)
        held = keep.astype(F32) + got.astype(F32)
        if step < bits - 1 or not last:
            held = held.astype(BF)
    return held.reshape(shape[:dim] + (-1,) + shape[dim + 1 :])


def by_source(pieces):
    member = lax.axis_index("head")
    level = [piece[None] for piece in pieces]
    bit = 0
    while len(level) > 1:
        level = [
            ordered_pair((member >> bit) & 1, level[at], level[at + 1], 0)
            for at in range(0, len(level), 2)
        ]
        bit += 1
    return level[0]


def body(
    latents,
    media,
    valid_counts,
    w_query,
    w_key,
    w_value,
    w_out,
    w_up,
    w_down,
    norm_gains,
    norm_biases,
    cotangent,
):
    groups = lax.axis_size("head")
    count = lax.axis_size("img")
    member = lax.axis_index("head")
    place = lax.axis_index("img")
    bits = bit_count(count)
    order_a = list(range(bits))
    order_b = [0] + list(range(bits - 1, 0, -1))
    gather_a = order_a[:0:-1] + [0]
    gather_b = order_b[:0:-1] + [0]
    total_images, patches, width = media.shape
    rows = latents.shape[1]
    images = total_images // groups
    local = w_query.shape[1]
    hidden_local = w_up.shape[1]
    scale = HEAD_DIM ** (-0.5)
    part = width // count

    def mine(values):
        return lax.dynamic_slice_in_dim(values, member * images, images, 0)

    attn_pack = jnp.concatenate([w_query, w_key, w_value, w_out], axis=1)
    attn_piece = lax.dynamic_slice_in_dim(attn_pack, place * part, part, 0)
    attn_got = jnp.concatenate([exchange(attn_piece, "head", j) for j in range(1, groups)], axis=1)
    half = attn_got.shape[1] // 2
    attn_all = jnp.concatenate(
        [attn_pack, gather_img(attn_got[:, :half], gather_a), gather_img(attn_got[:, half:], gather_b)],
        axis=1,
    ).reshape(width, groups, 4, local)
    up_piece = lax.dynamic_slice_in_dim(w_up, place * part, part, 0)
    down_piece = lax.dynamic_slice_in_dim(w_down, place * part, part, 0)
    ups, downs = [w_up], [w_down]
    for j in range(1, groups):
        ups.append(gather_img(exchange(up_piece, "head", j), gather_a))
        downs.append(gather_img(exchange(down_piece, "head", j), gather_b))

    latent_in = mine(latents).astype(F32)
    media_in = mine(media).astype(F32)
    upstream = mine(cotangent)
    counts = mine(valid_counts)
    media_hat, media_scale = layer_stats(media_in)
    latent_hat, latent_scale = layer_stats(latent_in)
    media_normed = (media_hat * norm_gains[0] + norm_biases[0]).astype(BF)
    latent_normed = (latent_hat * norm_gains[1] + norm_biases[1]).astype(BF)
    wide = groups * local
    wq, wk, wv, wo = (attn_all[:, :, at].reshape(width, wide) for at in range(4))
    w_kv = jnp.concatenate([wk, wv], axis=1)
    w_qkv = jnp.concatenate([wq, wk, wv], axis=1)

    def mm(a, b, dims):
        return lax.dot_general(a, b, (dims, ((), ())), preferred_element_type=F32)

    kv_media = mm(media_normed.reshape(-1, width), w_kv, ((1,), (0,))).astype(BF)
    qkv_lat = mm(latent_normed.reshape(-1, width), w_qkv, ((1,), (0,))).astype(BF)
    kv_media = kv_media.reshape(images, patches, 2 * wide)
    qkv_lat = qkv_lat.reshape(images, rows, 3 * wide)
    heads = wide // HEAD_DIM
    queries = qkv_lat[..., :wide].reshape(images, rows, heads, HEAD_DIM)
    kv = jnp.concatenate([kv_media, qkv_lat[..., wide:]], axis=1)
    key_rows = kv[..., :wide].reshape(images, patches + rows, heads, HEAD_DIM)
    value_rows = kv[..., wide:].reshape(images, patches + rows, heads, HEAD_DIM)
    positions = lax.iota(jnp.int32, patches + rows)
    allowed = (positions[None, :] < counts[:, None]) | (positions[None, :] >= patches)
    scores = jnp.einsum("ilhe,ikhe->ihlk", queries, key_rows, preferred_element_type=F32) * scale
    scores = jnp.where(allowed[:, None, None, :], scores, -1e30)
    attention = jax.nn.softmax(scores, axis=-1)
    attention_low = attention.astype(BF)
    attended = jnp.einsum("ihlk,ikhe->ilhe", attention_low, value_rows, preferred_element_type=F32)
    attended = attended.astype(BF).reshape(images * rows, wide)
    residual = latent_in.reshape(-1, width) + mm(attended, wo, ((1,), (1,)))
    res_hat, res_scale = layer_stats(residual)
    ffn_low = (res_hat * norm_gains[2] + norm_biases[2]).astype(BF)
    cot = upstream.reshape(-1, width)
    mlp = jnp.zeros(residual.shape, F32)
    grad_ffn = jnp.zeros(residual.shape, F32)
    ffn_grads = []
    for j in range(groups):
        pre = mm(ffn_low, ups[j], ((1,), (0,)))
        phi = 0.5 * (1.0 + lax.erf(pre * (0.5**0.5)))
        density = jnp.exp(-0.5 * pre * pre) * 0.3989422804014327
        hidden = (pre * phi).astype(BF)
        grad_pre = (mm(cot, downs[j], ((1,), (0,))) * (phi + pre * density)).astype(BF)
        mlp = mlp + mm(hidden, downs[j], ((1,), (1,)))
        grad_ffn = grad_ffn + mm(grad_pre, ups[j], ((1,), (1,)))
        up_grad = mm(ffn_low, grad_pre, ((0,), (0,))).astype(BF)
        down_grad = mm(cot, hidden, ((0,), (0,))).astype(BF)
        ffn_grads.append(
            (scatter_img(up_grad, order_a, 0, j == 0), scatter_img(down_grad, order_b, 0, j == 0))
        )
    out_mine = (residual + mlp).astype(BF).reshape(images, rows, width)
    latents_out = by_source(
        [out_mine] + [exchange(out_mine, "head", j) for j in range(1, groups)]
    ).reshape(total_images, rows, width)
    up_total = ffn_grads[0][0].astype(F32)
    down_total = ffn_grads[0][1].astype(F32)
    for j in range(1, groups):
        up_total = up_total + exchange(ffn_grads[j][0].astype(BF), "head", j).astype(F32)
        down_total = down_total + exchange(ffn_grads[j][1].astype(BF), "head", j).astype(F32)

    grad_residual = cot.astype(F32) + layer_back(grad_ffn, norm_gains[2], res_hat, res_scale)
    gain_ffn = jnp.sum(grad_ffn * res_hat, axis=0)
    bias_ffn = jnp.sum(grad_ffn, axis=0)
    grad_low = grad_residual.astype(BF)
    grad_wo = mm(grad_low, attended, ((0,), (0,)))
    grad_attended = mm(grad_low, wo, ((1,), (0,))).astype(BF).reshape(images, rows, heads, HEAD_DIM)
    grad_values = jnp.einsum(
        "ihlk,ilhe->ikhe", attention_low, grad_attended, preferred_element_type=F32
    )
    grad_attention = jnp.einsum(
        "ilhe,ikhe->ihlk", grad_attended, value_rows, preferred_element_type=F32
    )
    row_total = jnp.sum(attention * grad_attention, axis=-1, keepdims=True)
    grad_scores = (attention * (grad_attention - row_total)).astype(BF)
    grad_q = (
        jnp.einsum("ihlk,ikhe->ilhe", grad_scores, key_rows, preferred_element_type=F32) * scale
    )
    grad_k = jnp.einsum("ihlk,ilhe->ikhe", grad_scores, queries, preferred_element_type=F32) * scale
    grad_q = grad_q.astype(BF).reshape(images, rows, wide)
    grad_kv = jnp.concatenate(
        [
            grad_k.astype(BF).reshape(images, patches + rows, wide),
            grad_values.astype(BF).reshape(images, patches + rows, wide),
        ],
        axis=2,
    )
    media_gkv = grad_kv[:, :patches].reshape(-1, 2 * wide)
    latent_g = jnp.concatenate([grad_q, grad_kv[:, patches:]], axis=2).reshape(-1, 3 * wide)
    media_g = mm(media_gkv, w_kv, ((1,), (1,))).reshape(images, patches, width)
    latent_gn = mm(latent_g, w_qkv, ((1,), (1,))).reshape(images, rows, width)
    media_grad = layer_back(media_g, norm_gains[0], media_hat, media_scale).astype(BF)
    latents_grad = (
        grad_residual.reshape(images, rows, width)
        + layer_back(latent_gn, norm_gains[1], latent_hat, latent_scale)
    ).astype(BF)

    def spread(values):
        split = values.reshape(images, groups, -1, width)
        pieces = []
        for j in range(groups):
            piece = lax.dynamic_index_in_dim(split, member ^ j, 1, keepdims=False)
            pieces.append(piece if j == 0 else exchange(piece, "head", j))
        stacked = by_source(pieces)
        return stacked.reshape(total_images, -1, width)

    media_out = spread(media_grad)
    latents_back = spread(latents_grad)
    kv_wgrad = mm(media_normed.reshape(-1, width), media_gkv, ((0,), (0,)))
    qkv_wgrad = mm(latent_normed.reshape(-1, width), latent_g, ((0,), (0,)))
    all_wgrad = jnp.concatenate(
        [qkv_wgrad[:, :wide], qkv_wgrad[:, wide:] + kv_wgrad, grad_wo], axis=1
    ).astype(BF)
    all_wgrad = all_wgrad.reshape(width, 4, groups, local)
    attn_a = scatter_img(all_wgrad[:, :2], order_a, 0, False)
    attn_b = scatter_img(all_wgrad[:, 2:], order_b, 0, False)
    attn_sum = jnp.concatenate([attn_a, attn_b], axis=1)
    attn_total = attn_sum[:, :, 0].astype(F32)
    for j in range(1, groups):
        attn_total = attn_total + exchange(attn_sum[:, :, j], "head", j).astype(F32)

    norm_terms = jnp.stack(
        [
            jnp.sum(media_g * media_hat, axis=(0, 1)),
            jnp.sum(latent_gn * latent_hat, axis=(0, 1)),
            gain_ffn,
            jnp.sum(media_g, axis=(0, 1)),
            jnp.sum(latent_gn, axis=(0, 1)),
            bias_ffn,
        ]
    )
    for bit in range(bits):
        norm_terms = norm_terms + exchange(norm_terms, "img", 1 << bit)
    for bit in range(bit_count(groups)):
        norm_terms = norm_terms + exchange(norm_terms, "head", 1 << bit)
    share = width // (count * groups)
    norm_mine = lax.dynamic_slice_in_dim(norm_terms, (place * groups + member) * share, share, 1)
    return (
        latents_out,
        latents_back,
        media_out,
        attn_total[:, 0],
        attn_total[:, 1],
        attn_total[:, 2],
        attn_total[:, 3],
        up_total,
        down_total,
        norm_mine[:3],
        norm_mine[3:],
    )


def solution(mesh):
    return jax.shard_map(
        body,
        mesh=mesh,
        in_specs=(
            P("img", None, None),
            P("img", None, None),
            P("img"),
            P(None, "head"),
            P(None, "head"),
            P(None, "head"),
            P(None, "head"),
            P(None, "head"),
            P(None, "head"),
            P(),
            P(),
            P("img", None, None),
        ),
        out_specs=(
            P("img", None, None),
            P("img", "head", None),
            P("img", "head", None),
            P("img", "head"),
            P("img", "head"),
            P("img", "head"),
            P("img", "head"),
            P("img", "head"),
            P("img", "head"),
            P(None, ("img", "head")),
            P(None, ("img", "head")),
        ),
        check_vma=False,
    )
```
